32 devices in a mesh: ctx: 8 (over z, x), tp: 4 (over y, core).
Axes of the slice: x: 2, y: 2, z: 4, core: 2. Of those that a mesh axis runs over, the one named last changes fastest.
Arguments:
- gate_branch: bfloat16 [4096, 2048], P('tp', 'ctx'), may hold values from -6 to 6
- key_branch: bfloat16 [4096, 2048], P('tp', 'ctx'), may hold values from -6 to 6
- value_branch: bfloat16 [4096, 2048], P('tp', 'ctx'), may hold values from -6 to 6
- long_filter: bfloat16 [4096, 2048], P('tp', 'ctx'), may hold values from -0.125 to 0.125
- skip_gain: float32 [4096], P('tp'), may hold values from 0.25 to 2
- out_weight: bfloat16 [4096, 4096], P(None, 'tp'), may hold values from -0.09375 to 0.09375
Outputs:
- mixer_out: bfloat16 [4096, 2048], P('tp', 'ctx')
The draws below stay inside these ranges and needn't reach their ends.
All inputs are finite; a program needn't handle non-finite values.
Results may differ from the reference program's by a relative error of at most 0.013.
Values may be sent and summed in bfloat16 or wider, within the bound.
No kernel may reach another device: no remote copies, remote signals or barrier semaphores. Data moves between devices by JAX's collectives and lax.ppermute only.
A program may use at most 64 MiB of HBM per device.

```python
import math
import jax
import jax.numpy as jnp
from jax import lax

D = 4096
SEQ = 2048


def shard_levels(own_key, extent, shards, low, largest):
    level, own = 1.0, jax.random.fold_in(own_key, 6)
    for dim, blocks in shards:
        draws = jnp.exp(jax.random.uniform(jax.random.fold_in(own, dim), (blocks,), jnp.float32, low / len(shards), largest / len(shards)))
        level = level * jnp.repeat(draws, extent[dim] // blocks).reshape([-1 if axis == dim else 1 for axis in range(len(extent))])
    return level


def noise(stream_key, dims, spread, bound, shards=(), kind=jnp.bfloat16):
    entries = jax.random.normal(stream_key, dims, jnp.float32) * spread
    if len(shards) > 0:
        entries = shard_levels(stream_key, dims, shards, -0.22, 0.18) * entries
    return jnp.clip(entries, min=-bound, max=bound).astype(kind)


def setup_inputs(seed: int = 0) -> dict:
    key_list = jax.random.split(jax.random.key(seed), 7)
    return {
        "gate_branch": noise(key_list[0], (D, SEQ), 1.0, 6.0, ((0, 4), (1, 8))),
        "key_branch": noise(key_list[1], (D, SEQ), 1.0, 6.0, ((0, 4), (1, 8))),
        "value_branch": noise(key_list[2], (D, SEQ), 1.0, 6.0, ((0, 4), (1, 8))),
        "long_filter": noise(key_list[3], (D, SEQ), SEQ ** -0.5, 0.125, ((0, 4), (1, 8))),
        "skip_gain": jnp.clip(jnp.exp(math.log(2.0) - 2.0794415 * jax.random.uniform(key_list[4], (D,), jnp.float32) ** shard_levels(key_list[4], (D,), ((0, 4),), -0.2, 0.2)), 0.25, 2.0),
        "out_weight": noise(key_list[5], (D, D), D ** -0.5, 0.09375, ((1, 4),)),
    }


def causal_block(pair):
    mixed_rows, filter_rows = pair
    length = 2 * SEQ
    left_spec = jnp.fft.rfft(mixed_rows.astype(jnp.float32), n=length, axis=-1)
    right_spec = jnp.fft.rfft(filter_rows.astype(jnp.float32), n=length, axis=-1)
    result = jnp.fft.irfft(left_spec * right_spec, n=length, axis=-1)[:, :SEQ]
    return result.astype(jnp.bfloat16)


def reference(gate_branch, key_branch, value_branch, long_filter, skip_gain, out_weight):
    mixed = (key_branch.astype(jnp.float32) * value_branch.astype(jnp.float32)).astype(jnp.bfloat16)
    blocks = D // 128
    conv = lax.map(causal_block, (mixed.reshape(blocks, 128, SEQ), long_filter.reshape(blocks, 128, SEQ)))
    conv = conv.reshape(D, SEQ)
    gated = gate_branch.astype(jnp.float32) * (conv.astype(jnp.float32) + skip_gain[:, None] * mixed.astype(jnp.float32))
    gated = gated.astype(jnp.bfloat16)
    output = jnp.dot(out_weight.astype(jnp.float32), gated.astype(jnp.float32), preferred_element_type=jnp.float32)
    return output.astype(jnp.bfloat16)
```

```python
import functools
import math

import jax
import jax.numpy as jnp
import numpy as np
from jax import lax
from jax.experimental import pallas as pl
from jax.experimental.pallas import tpu as pltpu
from jax.sharding import PartitionSpec as P


VMEM = pltpu.VMEM
bf16 = jnp.bfloat16
f32 = jnp.float32


def whole_vmem():
    return pl.BlockSpec(memory_space=VMEM)


def scalars():
    return pl.BlockSpec(memory_space=pltpu.SMEM)


def odd_sums(x):
    size = len(x)
    if size == 1:
        return {0: (x[0], None)}
    if size == 2:
        return {1: (x[0], -x[1])}
    half = size // 2
    diff = {j: x[j] - x[size - j] for j in range(1, half)}
    both = {j: x[j] + x[size - j] for j in range(1, half)}
    found = {}
    for k in range(1, half, 2):
        cos = lambda j: math.cos(math.pi * j * k / size)
        sin = lambda j: math.sin(math.pi * j * k / size)
        even_re = x[0]
        for j in range(2, half, 2):
            even_re = even_re + diff[j] * cos(j)
        odd_re = sum((diff[j] * cos(j) for j in range(3, half, 2)), diff[1] * cos(1))
        even_im = x[half] if k % 4 == 1 else -x[half]
        for j in range(2, half, 2):
            even_im = even_im + both[j] * sin(j)
        odd_im = sum((both[j] * sin(j) for j in range(3, half, 2)), both[1] * sin(1))
        found[k] = (even_re + odd_re, -(odd_im + even_im))
        found[size - k] = (even_re - odd_re, even_im - odd_im)
    return found


def block_dft(x):
    n = len(x)
    out = {k: v for k, v in odd_sums(x).items()}
    step, rest = 2, list(x)
    while len(rest) > 1:
        half = len(rest) // 2
        low = [rest[j] - rest[j + half] for j in range(half)]
        for k, v in odd_sums(low).items():
            out[n if half == 1 else k * step] = v
        rest = [rest[j] + rest[j + half] for j in range(half)]
        step *= 2
    out[0] = (rest[0], None)
    return [out[k] for k in range(n + 1)]


def odd_sums_back(z, size):
    if size == 1:
        return [z[0][0]]
    if size == 2:
        return [z[1][0], -z[1][1]]
    half = size // 2
    ks = list(range(1, half, 2))
    re_sum = {k: z[k][0] + z[size - k][0] for k in ks}
    re_diff = {k: z[k][0] - z[size - k][0] for k in ks}
    im_sum = {k: z[k][1] + z[size - k][1] for k in ks}
    im_diff = {k: z[k][1] - z[size - k][1] for k in ks}
    out = [None] * size
    out[0] = functools.reduce(lambda a, b: a + b, [re_sum[k] for k in ks])
    out[half] = functools.reduce(
        lambda a, b: a + b, [im_diff[k] if k % 4 == 3 else -im_diff[k] for k in ks]
    )
    for j in range(1, half):
        re, im = (re_diff, im_sum) if j % 2 else (re_sum, im_diff)
        c = functools.reduce(
            lambda a, b: a + b, [re[k] * math.cos(math.pi * j * k / size) for k in ks]
        )
        s = functools.reduce(
            lambda a, b: a + b, [im[k] * math.sin(math.pi * j * k / size) for k in ks]
        )
        out[j] = c - s
        out[size - j] = -c - s
    return out


def block_dft_back(z):
    n = len(z) - 1
    acc, size, step = [z[0][0]], 1, n
    while size < n:
        part = odd_sums_back({0: z[n]} if size == 1 else {k: z[k * step] for k in range(1, size, 2)}, size)
        acc = [a + b for a, b in zip(acc, part)] + [a - b for a, b in zip(acc, part)]
        size *= 2
        step //= 2
    part = odd_sums_back({0: z[n]} if n == 1 else {k: z[k] for k in range(1, n, 2)}, n)
    return [a + b for a, b in zip(acc, part)]


def transform_table(length):
    turn = (np.arange(length)[:, None] * np.arange(length)[None, :]) % length
    angle = turn * (2.0 * np.pi / length)
    cos, sin = np.cos(angle), np.sin(angle)
    return np.block([[cos, -sin], [sin, cos]])


def twist_tables(n, length):
    total = 2 * n * length
    turn = (np.arange(n + 1)[:, None] * np.arange(length)[None, :]) % total
    angle = turn * (2.0 * np.pi / total)
    return np.stack([np.cos(angle), np.sin(angle)]).astype(np.float32)


def pack_kernel(n, me_ref, key_ref, value_ref, filter_ref, *outs):
    me = me_ref[0]
    rows = key_ref.shape[0] // n
    for k in range(n):
        at = pl.ds(pl.multiple_of((me ^ k) * rows, rows), rows)
        outs[k][0] = (key_ref[at, :].astype(f32) * value_ref[at, :].astype(f32)).astype(bf16)
        outs[k][1] = filter_ref[at, :]


def conv_kernel(n, me_ref, table_ref, twist_ref, *refs):
    blocks, outs = refs[:n], refs[n : 2 * n]
    timed, spec, back, done = refs[2 * n :]
    me = me_ref[0]
    rows, length = outs[0].shape
    total = 2 * n * length
    tile, lanes = 16, 128
    for k in range(n):
        timed[me ^ k] = blocks[k][...]

    def twist(k, lane):
        return (
            twist_ref[0, k : k + 1, lane : lane + lanes],
            twist_ref[1, k : k + 1, lane : lane + lanes],
        )

    for side in range(2):
        for lane in range(0, length, lanes):

            @pl.loop(0, rows // tile)
            def _(step):
                at = pl.ds(pl.multiple_of(step * tile, tile), tile)
                to = pl.ds(pl.multiple_of(side * rows + step * tile, tile), tile)
                x = [timed[j, side, at, lane : lane + lanes].astype(f32) for j in range(n)]
                for k, (re, im) in enumerate(block_dft(x)):
                    if k == 0:
                        out_re, out_im = re, jnp.zeros_like(re)
                    else:
                        cos, sin = twist(k, lane)
                        if im is None:
                            out_re, out_im = re * cos, -re * sin
                        else:
                            out_re, out_im = re * cos + im * sin, im * cos - re * sin
                    spec[k, to, lane : lane + lanes] = out_re.astype(bf16)
                    spec[k, to, length + lane : length + lane + lanes] = out_im.astype(bf16)

    @pl.loop(0, n + 1)
    def _(k):
        both = jnp.dot(spec[k], table_ref[...], preferred_element_type=f32)
        xr, xi = both[:rows, :length], both[:rows, length:]
        hr, hi = both[rows:, :length], both[rows:, length:]
        prod = jnp.concatenate([xr * hr - xi * hi, -(xr * hi + xi * hr)], axis=1)
        back[k] = jnp.dot(prod.astype(bf16), table_ref[...], preferred_element_type=f32)

    for lane in range(0, length, lanes):

        @pl.loop(0, rows // tile)
        def _(step):
            at = pl.ds(pl.multiple_of(step * tile, tile), tile)
            z = []
            for k in range(n + 1):
                re = back[k, at, lane : lane + lanes]
                im = back[k, at, length + lane : length + lane + lanes]
                if k == 0:
                    z.append((re * (1.0 / total), None))
                    continue
                cos, sin = twist(k, lane)
                scale = (1.0 if k == n else 2.0) / total
                cos, sin = cos * scale, sin * scale
                z.append((re * cos + im * sin, None if k == n else re * sin - im * cos))
            for j, y in enumerate(block_dft_back(z)):
                done[j, at, lane : lane + lanes] = y.astype(bf16)

    for k in range(n):
        outs[k][...] = done[me ^ k]


def gate_kernel(n, me_ref, gate_ref, key_ref, value_ref, skip_ref, *refs):
    convs, out_ref = refs[:n], refs[n]
    me = me_ref[0]
    rows = convs[0].shape[0]
    for k in range(n):
        at = pl.ds(pl.multiple_of((me ^ k) * rows, rows), rows)
        mixed = (key_ref[at, :].astype(f32) * value_ref[at, :].astype(f32)).astype(bf16)
        inner = convs[k][...].astype(f32) + skip_ref[at, :] * mixed.astype(f32)
        out_ref[at, :] = (gate_ref[at, :].astype(f32) * inner).astype(bf16)


def proj_kernel(pick_ref, weight_ref, gated_ref, *refs):
    adds, out_ref = refs[:-1], refs[-1]
    acc = jnp.dot(weight_ref[...], gated_ref[...], preferred_element_type=f32)
    for add in adds:
        acc = acc + add[...].astype(f32)
    out_ref[...] = acc.astype(out_ref.dtype)


def project(pick, weight, gated, adds, rows, tile, dtype):
    depth, cols = gated.shape
    count = rows // tile
    block = pl.BlockSpec((tile, cols), lambda i, pick: (i, 0))
    return pl.pallas_call(
        proj_kernel,
        grid_spec=pltpu.PrefetchScalarGridSpec(
            num_scalar_prefetch=1,
            grid=(count,),
            in_specs=[
                pl.BlockSpec((tile, depth), lambda i, pick: (pick[0] * count + i, 0)),
                pl.BlockSpec((depth, cols), lambda i, pick: (0, 0)),
            ]
            + [block] * len(adds),
            out_specs=block,
        ),
        out_shape=jax.ShapeDtypeStruct((rows, cols), dtype),
        compiler_params=pltpu.CompilerParams(vmem_limit_bytes=16 * 2**20),
        cost_estimate=pl.CostEstimate(
            flops=2 * rows * depth * cols,
            bytes_accessed=2 * rows * depth,
            transcendentals=0,
        ),
    )(pick, weight, gated, *adds)


def xor_pairs(size, k):
    return [(i, i ^ k) for i in range(size)]


def body(n, tp, gate_branch, key_branch, value_branch, long_filter, skip_gain, out_weight):
    channels, length = key_branch.shape
    rows = channels // n
    me = lax.axis_index("ctx").astype(jnp.int32).reshape(1)
    mine = lax.axis_index("tp").astype(jnp.int32)
    table = jnp.asarray(transform_table(length), bf16)
    twists = jnp.asarray(twist_tables(n, length))
    limit = pltpu.CompilerParams(vmem_limit_bytes=24 * 2**20)

    packed = pl.pallas_call(
        functools.partial(pack_kernel, n),
        in_specs=[scalars()] + [whole_vmem()] * 3,
        out_specs=[whole_vmem()] * n,
        out_shape=[jax.ShapeDtypeStruct((2, rows, length), bf16)] * n,
        compiler_params=limit,
    )(me, key_branch, value_branch, long_filter)
    arrived = [packed[0]] + [
        lax.ppermute(packed[k], "ctx", xor_pairs(n, k)) for k in range(1, n)
    ]
    convolved = pl.pallas_call(
        functools.partial(conv_kernel, n),
        in_specs=[scalars()] + [whole_vmem()] * (n + 2),
        out_specs=[whole_vmem()] * n,
        out_shape=[jax.ShapeDtypeStruct((rows, length), bf16)] * n,
        scratch_shapes=[
            VMEM((n, 2, rows, length), bf16),
            VMEM((n + 1, 2 * rows, 2 * length), bf16),
            VMEM((n + 1, rows, 2 * length), f32),
            VMEM((n, rows, length), bf16),
        ],
        compiler_params=limit,
    )(me, table, twists, *arrived)
    returned = [convolved[0]] + [
        lax.ppermute(convolved[k], "ctx", xor_pairs(n, k)) for k in range(1, n)
    ]
    gated = pl.pallas_call(
        functools.partial(gate_kernel, n),
        in_specs=[scalars()] + [whole_vmem()] * (n + 4),
        out_specs=whole_vmem(),
        out_shape=jax.ShapeDtypeStruct((channels, length), bf16),
        compiler_params=limit,
    )(me, gate_branch, key_branch, value_branch, skip_gain[:, None], *returned)

    share = out_weight.shape[0] // tp
    tile = min(256, share)

    def part(k, adds, dtype=bf16):
        return project((mine ^ k).reshape(1), out_weight, gated, adds, share, tile, dtype)

    extra = {k: [] for k in range(tp)}
    bit = 1
    while bit < tp:
        for k in range(tp - 1, -1, -1):
            if k & bit and not k & (bit - 1):
                block = part(k, extra[k])
                extra[k ^ bit].append(lax.ppermute(block, "tp", xor_pairs(tp, bit)))
        bit *= 2
    return part(0, extra[0])


def solution(mesh):
    placed = (
        P("tp", "ctx"),
        P("tp", "ctx"),
        P("tp", "ctx"),
        P("tp", "ctx"),
        P("tp"),
        P(None, "tp"),
    )
    return jax.shard_map(
        functools.partial(body, mesh.shape["ctx"], mesh.shape["tp"]),
        mesh=mesh,
        in_specs=placed,
        out_specs=P("tp", "ctx"),
        check_vma=False,
    )
```
